512 devices in a mesh: space: 128 (over x, y, z_lo, core), band: 4 (over z_hi).
Axes of the slice: x: 4, y: 8, z: 8 (z_hi: 4, z_lo: 2; z = z_hi * 2 + z_lo), core: 2. Of those that a mesh axis runs over, the one named last changes fastest.
Arguments:
- states_in: bfloat16 [256, 262144], P('band', 'space'), may hold values from -6 to 6
- kinetic: bfloat16 [64, 64], replicated, may hold values from -0.75 to 0.75
- cell_scale: float32 [32768], P('space'), may hold values from 0.5 to 2
- cell_nodes: int32 [64, 32768], P(None, 'space'), may hold values from 0 to 4095
- boundary: int32 [65536], P('space'), may hold values from 0 to 2047, as said below
- potential: float32 [262144], P('space'), may hold values from -2 to 2
- inv_mass_root: float32 [262144], P('space'), may hold values from 0.2 to 1.875
Outputs:
- filtered: bfloat16 [256, 262144], P('band', 'space')
- margin: float32 [256, 256], P('band')
The draws below stay inside these ranges and needn't reach their ends.
Inputs may be any that keep to these rules, and one draw needn't show every extreme that they name: `boundary`: each partition's 512 entries are distinct node numbers of that partition. `cell_nodes`: A value below 2048 is a node of the cell's own partition; a value 2048 + j * 512 + b is entry b of the boundary list of the partition whose space index is the cell's own plus (-2, -1, 1, 2)[j], taken modulo the number of partitions.
All inputs are finite; a program needn't handle non-finite values.
Results may differ from the reference program's by a relative error of at most 0.0095.
Values may be sent and summed in bfloat16 or wider, within the bound.
No kernel may reach another device: no remote copies, remote signals or barrier semaphores. Data moves between devices by JAX's collectives and lax.ppermute only.
A program may use at most 64 MiB of HBM per device.

```python
import math
import jax
import jax.numpy as jnp
from jax import lax

STATES = 256
CELL_NODES = 64
N_DEV = 2048
C_DEV = 256
NB = 512
NODES = 262144
CELLS = 32768
N_SPACE = 128
N_BAND = 4


def draw_boundary(key, part):
    keys = jax.random.split(jax.random.fold_in(key, 11), N_SPACE)
    lists = jax.vmap(lambda single: jax.random.permutation(single, N_DEV)[:NB])(keys)
    return lists.reshape(-1).astype(jnp.int32)


def draw_inv_mass_root(key, part):
    position = jnp.arange(NODES, dtype=jnp.float32) / NODES
    rough = jnp.exp(jax.random.uniform(jax.random.fold_in(key, 23), (NODES,), jnp.float32, jnp.log(0.8), jnp.log(1.25)))
    grade = 0.4 * jnp.power(3.0, position)
    return (grade * rough).astype(jnp.float32)


def place_ends(result, key, least, largest):
    longest = result.shape.index(max(result.shape))
    spots = []
    for shift in (0, 1):
        where = [jax.random.randint(jax.random.fold_in(key, axis), (), 0, length) for axis, length in enumerate(result.shape)]
        where[longest] = (where[longest] + shift) % result.shape[longest]
        spots.append(tuple(where))
    return result.at[spots[0]].set(least).at[spots[1]].set(largest)


def shard_levels(rng, extent, cuts, least, top_value):
    factor_of = 1.0
    for axis_at, shards_of in cuts:
        heights = jax.random.uniform(jax.random.fold_in(jax.random.fold_in(rng, 6), axis_at), (shards_of,), jnp.float32, least / len(cuts), top_value / len(cuts))
        factor_of = factor_of * jnp.repeat(jnp.exp(heights), extent[axis_at] // shards_of).reshape((-1,) + (1,) * (len(extent) - 1 - axis_at))
    return factor_of


def noise(stream_key, extent, deviation, limit, cuts=(), held_as=jnp.bfloat16):
    factor_of = shard_levels(stream_key, extent, cuts, -0.22, 0.18) if cuts else 1.0
    result = jax.random.normal(stream_key, extent, jnp.float32) * deviation * factor_of
    return jnp.minimum(jnp.maximum(result, -limit), limit).astype(held_as)


def setup_inputs(seed: int = 0) -> dict:
    streams_of = jax.random.split(jax.random.key(seed), 8)
    return {
        "states_in": noise(streams_of[0], (STATES, NODES), 1.0, 6.0, ((0, 4), (1, 128))),
        "kinetic": noise(streams_of[1], (CELL_NODES, CELL_NODES), CELL_NODES ** -0.5, 0.75),
        "cell_scale": jnp.clip(jnp.exp(math.log(2.0) - 1.3862944 * jax.random.uniform(streams_of[2], (CELLS,), jnp.float32) ** shard_levels(streams_of[2], (CELLS,), ((0, 128),), -0.2, 0.2)), 0.5, 2.0),
        "cell_nodes": place_ends(jax.random.randint(streams_of[3], (CELL_NODES, CELLS), 0, N_DEV + 4 * NB), jax.random.fold_in(streams_of[3], 1), 0, (N_DEV + 4 * NB) - 1).astype(jnp.int32),
        "boundary": draw_boundary(jax.random.fold_in(streams_of[7], 71), 0),
        "potential": jnp.clip(jax.random.uniform(streams_of[5], (NODES,), jnp.float32, -2.0, 2.0) * shard_levels(streams_of[5], (NODES,), ((0, 128),), -0.4, 0.0), -2.0, 2.0),
        "inv_mass_root": draw_inv_mass_root(jax.random.fold_in(streams_of[7], 71), 0),
    }


OFFSETS = (-2, -1, 1, 2)
CENTER = 0.5
HALF = 6.0


def global_ids(cell_nodes, boundary):
    cell_count = cell_nodes.shape[1]
    owner = (jnp.arange(cell_count, dtype=jnp.int32) // C_DEV).astype(jnp.int32)[None, :]
    ghost = jnp.maximum(cell_nodes - N_DEV, 0)
    slot_index = ghost // NB
    entry = ghost % NB
    shifts = jnp.array(OFFSETS, dtype=jnp.int32)[slot_index]
    source = (owner + shifts) % N_SPACE
    remote = source * N_DEV + boundary[source * NB + entry]
    return jnp.where(cell_nodes < N_DEV, owner * N_DEV + cell_nodes, remote).astype(jnp.int32)


def apply_operator(values, kinetic, id_blocks, scale_blocks, potential, inv_root):
    width = values.shape[1]
    scaled = (inv_root[:, None] * values.astype(jnp.float32)).astype(jnp.bfloat16)
    kinetic_f = kinetic.astype(jnp.float32)

    def add_cells(totals, item):
        indices, scales_here = item
        gathered = scaled[indices].astype(jnp.float32)
        terms = jnp.einsum('ij,jcs->ics', kinetic_f, gathered) * scales_here[None, :, None]
        totals = totals.at[indices.reshape(-1)].add(terms.reshape(-1, width))
        return totals, None

    totals = lax.scan(add_cells, jnp.zeros((values.shape[0], width), jnp.float32), (id_blocks, scale_blocks))[0]
    return inv_root[:, None] * (totals + potential[:, None] * scaled.astype(jnp.float32))


def reference(states_in, kinetic, cell_scale, cell_nodes, boundary, potential, inv_mass_root):
    ids = global_ids(cell_nodes, boundary)
    id_blocks = ids.reshape(CELL_NODES, N_SPACE, C_DEV).transpose(1, 0, 2)
    scale_blocks = cell_scale.reshape(N_SPACE, C_DEV)
    block_rows = STATES // N_BAND
    seconds = []
    outputs = []
    for block in range(N_BAND):
        start_v = states_in[block * block_rows:(block + 1) * block_rows].T
        image = apply_operator(start_v, kinetic, id_blocks, scale_blocks, potential, inv_mass_root)
        first = ((image - CENTER * start_v.astype(jnp.float32)) / HALF).astype(jnp.bfloat16)
        image_two = apply_operator(first, kinetic, id_blocks, scale_blocks, potential, inv_mass_root)
        second = 2.0 * (image_two - CENTER * first.astype(jnp.float32)) / HALF - start_v.astype(jnp.float32)
        seconds.append(second.T)
        outputs.append(second.T.astype(jnp.bfloat16))
    filtered = jnp.concatenate(outputs, axis=0)
    rows_list = []
    for left in seconds:
        pieces = [lax.dot_general(left, right, (((1,), (1,)), ((), ())), precision=lax.Precision.HIGHEST, preferred_element_type=jnp.float32) for right in seconds]
        rows_list.append(jnp.concatenate(pieces, axis=1))
    margin = jnp.concatenate(rows_list, axis=0) / NODES
    return filtered, margin
```

```python
import jax
import jax.numpy as jnp
from jax import lax
from jax.experimental import pallas as pl
from jax.experimental.pallas import tpu as pltpu
from jax.sharding import Mesh
from jax.sharding import PartitionSpec as P

SPACE = ("space_0", "space_1", "space_2", "space_3")
OFFSETS = (-2, -1, 1, 2)
CENTER = 0.5
HALF = 6.0
TILE = 256
STEP = 1024
BF = jnp.bfloat16
F32 = jnp.float32


def from_behind(x, axis, by):
    count = lax.axis_size(axis)
    return lax.ppermute(x, axis, [(i, (i + by) % count) for i in range(count)])


def selection(index, base, count):
    width = index.shape[1]
    high = index // TILE
    low = (index % TILE).astype(F32)
    lines = lax.broadcasted_iota(jnp.int32, (TILE, width), 0).astype(F32).astype(BF)
    tiles = []
    for tile in range(count // TILE):
        here = jnp.where(high == base // TILE + tile, low, -1.0).astype(BF)
        tiles.append(jnp.where(lines == here, jnp.ones((), BF), jnp.zeros((), BF)))
    return jnp.concatenate(tiles, axis=0)


def picked(values, chosen):
    return jnp.dot(values, chosen, preferred_element_type=F32)


def put_back(values, chosen):
    return lax.dot_general(values, chosen, (((1,), (1,)), ((), ())), preferred_element_type=F32)


def prepare_kernel(values, inv_root, boundary, scaled_ref, rim_ref):
    scaled = (inv_root[...] * values[...].astype(F32)).astype(BF)
    scaled_ref[...] = scaled
    chosen = selection(boundary[...], 0, scaled.shape[1])
    rim_ref[...] = picked(scaled, chosen).astype(BF)


def prepare(values, inv_root, boundary):
    rows, owned = values.shape
    return pl.pallas_call(
        prepare_kernel,
        out_shape=(
            jax.ShapeDtypeStruct((rows, owned), BF),
            jax.ShapeDtypeStruct((rows, boundary.shape[1]), BF),
        ),
        name="prepare",
    )(values, inv_root, boundary)


def cells_kernel(owned, index, scale, kinetic, table, out_ref, rim_ref, acc):
    step = pl.program_id(0)
    chosen = selection(index[...], 0, table.shape[1])
    gathered = picked(table[...], chosen).astype(BF)
    terms = jnp.concatenate(
        [
            jnp.dot(gathered[:, i : i + TILE], kinetic[...], preferred_element_type=F32)
            for i in range(0, gathered.shape[1], TILE)
        ],
        axis=1,
    )
    terms = (terms * scale[...]).astype(BF)
    part = put_back(terms, chosen)

    @pl.when(step == 0)
    def _():
        acc[...] = part

    @pl.when(step > 0)
    def _():
        acc[...] += part

    @pl.when(step == pl.num_programs(0) - 1)
    def _():
        out_ref[...] = acc[:, :owned]
        rim_ref[...] = acc[:, owned:].astype(BF)


def cells(table, owned, index, scale, kinetic):
    rows, nodes = table.shape
    places = index.shape[1]
    line = pl.BlockSpec((1, STEP), lambda i: (0, i))

    def kernel(*refs):
        cells_kernel(owned, *refs)

    return pl.pallas_call(
        kernel,
        grid=(places // STEP,),
        in_specs=[
            line,
            line,
            pl.BlockSpec(kinetic.shape, lambda i: (0, 0)),
            pl.BlockSpec((rows, nodes), lambda i: (0, 0)),
        ],
        out_specs=(
            pl.BlockSpec((rows, owned), lambda i: (0, 0)),
            pl.BlockSpec((rows, nodes - owned), lambda i: (0, 0)),
        ),
        out_shape=(
            jax.ShapeDtypeStruct((rows, owned), F32),
            jax.ShapeDtypeStruct((rows, nodes - owned), BF),
        ),
        scratch_shapes=[pltpu.VMEM((rows, nodes), F32)],
        name="cells",
    )(index, scale, kinetic, table)


def image_of(own, arrived, scaled, inv_root, potential, chosen):
    back = arrived[0][...].astype(F32)
    for part in arrived[1:]:
        back = back + part[...].astype(F32)
    upper = back.astype(BF)
    lower = (back - upper.astype(F32)).astype(BF)
    both = put_back(jnp.concatenate([upper, lower], axis=0), chosen)
    rows = back.shape[0]
    total = own[...] + both[:rows] + both[rows:]
    return inv_root[...] * (total + potential[...] * scaled[...].astype(F32))


def first_kernel(own, a0, a1, a2, a3, scaled, start, inv_root, potential, boundary, first_ref, scaled_ref, rim_ref):
    chosen = selection(boundary[...], 0, own.shape[1])
    image = image_of(own, (a0, a1, a2, a3), scaled, inv_root, potential, chosen)
    first = ((image - CENTER * start[...].astype(F32)) / HALF).astype(BF)
    first_ref[...] = first
    scaled_new = (inv_root[...] * first.astype(F32)).astype(BF)
    scaled_ref[...] = scaled_new
    rim_ref[...] = picked(scaled_new, chosen).astype(BF)


def second_kernel(own, a0, a1, a2, a3, scaled, start, first, inv_root, potential, boundary, out_ref):
    chosen = selection(boundary[...], 0, own.shape[1])
    image = image_of(own, (a0, a1, a2, a3), scaled, inv_root, potential, chosen)
    second = 2.0 * (image - CENTER * first[...].astype(F32)) / HALF - start[...].astype(F32)
    out_ref[...] = second.astype(BF)


def exchange_out(rim):
    return [from_behind(rim, SPACE, -offset) for offset in OFFSETS]


def exchange_back(ghost, width):
    return [
        from_behind(ghost[:, i * width : (i + 1) * width], SPACE, offset)
        for i, offset in enumerate(OFFSETS)
    ]


def in_blocks(x, dim, count):
    dims = x.shape
    blocks = x.reshape(*dims[:dim], count, dims[dim] // count, *dims[dim + 1 :])
    return jnp.moveaxis(blocks, dim, 0)


def body(states_in, kinetic, cell_scale, cell_nodes, boundary, potential, inv_mass_root):
    nodes_per_cell = kinetic.shape[0]
    rows, owned = states_in.shape
    width = boundary.shape[0]
    index = cell_nodes.T.reshape(1, -1)
    scale = jnp.repeat(cell_scale, nodes_per_cell).reshape(1, -1)
    stacked = jnp.kron(jnp.eye(TILE // nodes_per_cell, dtype=BF), kinetic.T)
    inv_root = inv_mass_root[None]
    potential = potential[None]
    boundary = boundary[None]

    scaled, rim = prepare(states_in, inv_root, boundary)
    table = jnp.concatenate([scaled, *exchange_out(rim)], axis=1)
    own, ghost = cells(table, owned, index, scale, stacked)
    arrived = exchange_back(ghost, width)
    first, scaled, rim = pl.pallas_call(
        first_kernel,
        out_shape=(
            jax.ShapeDtypeStruct((rows, owned), BF),
            jax.ShapeDtypeStruct((rows, owned), BF),
            jax.ShapeDtypeStruct((rows, width), BF),
        ),
        name="first",
    )(own, *arrived, scaled, states_in, inv_root, potential, boundary)
    table = jnp.concatenate([scaled, *exchange_out(rim)], axis=1)
    own, ghost = cells(table, owned, index, scale, stacked)
    arrived = exchange_back(ghost, width)
    filtered = pl.pallas_call(
        second_kernel,
        out_shape=jax.ShapeDtypeStruct((rows, owned), BF),
        name="second",
    )(own, *arrived, scaled, states_in, first, inv_root, potential, boundary)

    node_total = owned * lax.axis_size(SPACE)
    regrouped = lax.all_to_all(filtered, "band", split_axis=1, concat_axis=0, tiled=True)
    partial_sum = lax.dot_general(regrouped, regrouped, (((1,), (1,)), ((), ())), preferred_element_type=F32)
    blocks = in_blocks(partial_sum.astype(BF), 0, lax.axis_size("band"))
    reduced = jnp.sum(lax.all_to_all(blocks, "band", 0, 0, tiled=True).astype(F32), axis=0)
    margin = lax.psum(reduced, SPACE) / node_total
    return filtered, margin


def solution(mesh):
    split = Mesh(
        mesh.devices.reshape(4, 8, 2, 2, mesh.shape["band"]),
        ("space_0", "space_1", "space_2", "space_3", "band"),
    )
    in_specs = (P("band", SPACE), P(), P(SPACE), P(None, SPACE), P(SPACE), P(SPACE), P(SPACE))
    out_specs = (P("band", SPACE), P("band", None))
    return jax.shard_map(body, mesh=split, in_specs=in_specs, out_specs=out_specs, check_vma=False)
```

```python
import jax
import jax.numpy as jnp
from jax import lax
from jax.experimental import pallas as pl
from jax.experimental.pallas import tpu as pltpu
from jax.sharding import Mesh
from jax.sharding import PartitionSpec as P

SPACE = ("outer", "quad")
QUAD = 4
OFFSETS = (-2, -1, 1, 2)
CENTER = 0.5
HALF = 6.0
TILE = 256
STEP = 2048
BF = jnp.bfloat16
F32 = jnp.float32


def selection(low, count):
    width = low.shape[1]
    lines = lax.broadcasted_iota(jnp.int32, (TILE, width), 0).astype(F32).astype(BF)
    place = (low % TILE).astype(F32)
    tiles = []
    for tile in range(count // TILE):
        here = jnp.where(low // TILE == tile, place, -1.0).astype(BF)
        tiles.append(jnp.where(lines == here, jnp.ones((), BF), jnp.zeros((), BF)))
    return jnp.concatenate(tiles, axis=0)


def picked(values, chosen):
    return jnp.dot(values, chosen, preferred_element_type=F32)


def put_back(values, chosen):
    return lax.dot_general(values, chosen, (((1,), (1,)), ((), ())), preferred_element_type=F32)


def from_pieces(values, piece, count):
    return jnp.concatenate([values[:, i * piece : (i + 1) * piece] for i in range(count)], axis=0)


def take_columns(values, index, piece):
    rows, count = values.shape[0], values.shape[1] // piece
    both = picked(from_pieces(values, piece, count), selection(index % piece, piece))
    part = index // piece
    result = both[:rows]
    for i in range(1, count):
        result = jnp.where(part == i, both[i * rows : (i + 1) * rows], result)
    return result


def add_columns(values, index, piece, count):
    rows = values.shape[0]
    part = index // piece
    none = jnp.zeros((), values.dtype)
    spread = jnp.concatenate([jnp.where(part == i, values, none) for i in range(count)], axis=0)
    sums = put_back(spread, selection(index % piece, piece))
    return [sums[i * rows : (i + 1) * rows] for i in range(count)]


def prepare_kernel(values, inv_root, boundary, scaled_ref, rim_ref):
    scaled = (inv_root[...] * values[...].astype(F32)).astype(BF)
    scaled_ref[...] = scaled
    rim_ref[...] = take_columns(scaled, boundary[...], boundary.shape[1]).astype(BF)


def cells_kernel(index, scale, kinetic, scaled, ghosts, own_ref, ghost_ref, table, acc):
    step = pl.program_id(0)
    count, rows, piece = ghosts.shape
    own_count = scaled.shape[1] // piece

    @pl.when(step == 0)
    def _():
        for i in range(own_count):
            table[i * rows : (i + 1) * rows] = scaled[:, i * piece : (i + 1) * piece]
        for i in range(count):
            table[(own_count + i) * rows : (own_count + i + 1) * rows] = ghosts[i]

    places = index[...]
    chosen = selection(places % piece, piece)
    part = places // piece
    both = picked(table[...], chosen)
    gathered = both[:rows]
    for i in range(1, own_count + count):
        gathered = jnp.where(part == i, both[i * rows : (i + 1) * rows], gathered)
    gathered = gathered.astype(BF)
    terms = jnp.concatenate(
        [
            jnp.dot(gathered[:, i : i + TILE], kinetic[...], preferred_element_type=F32)
            for i in range(0, gathered.shape[1], TILE)
        ],
        axis=1,
    )
    terms = terms * scale[...]
    spread = jnp.concatenate(
        [jnp.where(part == i, terms, 0.0).astype(BF) for i in range(own_count + count)], axis=0
    )
    sums = put_back(spread, chosen)

    @pl.when(step == 0)
    def _():
        acc[...] = sums

    @pl.when(step > 0)
    def _():
        acc[...] += sums

    @pl.when(step == pl.num_programs(0) - 1)
    def _():
        for i in range(own_count):
            own_ref[:, i * piece : (i + 1) * piece] = acc[i * rows : (i + 1) * rows]
        for i in range(count):
            ghost_ref[i] = acc[(own_count + i) * rows : (own_count + i + 1) * rows].astype(BF)


def cells(scaled, ghosts, index, scale, kinetic):
    rows, owned = scaled.shape
    count, _, piece = ghosts.shape
    places = index.shape[1]
    line = pl.BlockSpec((1, STEP), lambda i: (0, i))
    stack = (owned // piece + count) * rows
    return pl.pallas_call(
        cells_kernel,
        grid=(places // STEP,),
        in_specs=[
            line,
            line,
            pl.BlockSpec(kinetic.shape, lambda i: (0, 0)),
            pl.BlockSpec(scaled.shape, lambda i: (0, 0)),
            pl.BlockSpec(ghosts.shape, lambda i: (0, 0, 0)),
        ],
        out_specs=(
            pl.BlockSpec((rows, owned), lambda i: (0, 0)),
            pl.BlockSpec(ghosts.shape, lambda i: (0, 0, 0)),
        ),
        out_shape=(
            jax.ShapeDtypeStruct((rows, owned), F32),
            jax.ShapeDtypeStruct(ghosts.shape, BF),
        ),
        scratch_shapes=[pltpu.VMEM((stack, piece), BF), pltpu.VMEM((stack, piece), F32)],
        name="cells",
    )(index, scale, kinetic, scaled, ghosts)


def image_of(own, arrived, scaled, inv_root, potential, boundary):
    back = arrived[0].astype(F32)
    for i in range(1, arrived.shape[0]):
        back = back + arrived[i].astype(F32)
    upper = back.astype(BF)
    lower = (back - upper.astype(F32)).astype(BF)
    rows, piece = back.shape
    sums = add_columns(jnp.concatenate([upper, lower], axis=0), boundary[...], piece, own.shape[1] // piece)
    total = own[...] + jnp.concatenate([part[:rows] + part[rows:] for part in sums], axis=1)
    return inv_root[...] * (total + potential[...] * scaled[...].astype(F32))


def first_kernel(own, arrived, scaled, start, inv_root, potential, boundary, first_ref, scaled_ref, rim_ref):
    image = image_of(own, arrived, scaled, inv_root, potential, boundary)
    first = ((image - CENTER * start[...].astype(F32)) / HALF).astype(BF)
    first_ref[...] = first
    scaled_new = (inv_root[...] * first.astype(F32)).astype(BF)
    scaled_ref[...] = scaled_new
    rim_ref[...] = take_columns(scaled_new, boundary[...], boundary.shape[1]).astype(BF)


def second_kernel(own, arrived, scaled, start, first, inv_root, potential, boundary, out_ref):
    image = image_of(own, arrived, scaled, inv_root, potential, boundary)
    second = 2.0 * (image - CENTER * first[...].astype(F32)) / HALF - start[...].astype(F32)
    out_ref[...] = second.astype(BF)


def across(x):
    quads = lax.axis_size(SPACE[0])
    pairs = []
    for m in range(quads):
        for r in range(QUAD):
            other = (m + 1) % quads if r >= 2 else (m - 1) % quads
            pairs.append((m * QUAD + r, other * QUAD + (r + 2) % QUAD))
    return lax.ppermute(x, SPACE, pairs)


def exchange_out(rim):
    mine = lax.axis_index(SPACE[1])
    near = lax.all_gather(rim, SPACE[1], axis=0)
    edge = lax.dynamic_slice_in_dim(near, jnp.where(mine >= 2, 2, 0), 2, axis=0)
    far = across(edge)
    low = mine < 2
    line = jnp.concatenate([far, near, far], axis=0)
    parts = [lax.dynamic_index_in_dim(line, mine + 2 + offset, 0, keepdims=False) for offset in OFFSETS]
    return jnp.stack(parts)


def exchange_back(ghost):
    mine = lax.axis_index(SPACE[1])
    low = mine < 2
    direct = jnp.where(low, ghost[0], ghost[3])
    handed = jnp.where(mine == 0, ghost[1], jnp.where(mine == 3, ghost[2], jnp.zeros_like(direct)))
    arrived = across(jnp.stack([direct, handed]))
    zero = jnp.zeros_like(direct)
    blocks = []
    for member in range(QUAD):
        block = zero
        for i, offset in enumerate(OFFSETS):
            block = jnp.where(mine + offset == member, ghost[i], block)
        blocks.append(block)
    blocks = jnp.stack(blocks)
    extra = jnp.where(jnp.arange(QUAD)[:, None, None] == jnp.where(mine == 1, 0, jnp.where(mine == 2, 3, -1)), arrived[1][None], 0)
    blocks = (blocks.astype(F32) + extra.astype(F32)).astype(BF)
    near = lax.all_to_all(blocks, SPACE[1], 0, 0, tiled=True)
    return jnp.concatenate([near, arrived[:1]], axis=0)


def body(states_in, kinetic, cell_scale, cell_nodes, boundary, potential, inv_mass_root):
    nodes_per_cell = kinetic.shape[0]
    rows, owned = states_in.shape
    index = cell_nodes.T.reshape(1, -1)
    scale = jnp.repeat(cell_scale, nodes_per_cell).reshape(1, -1)
    stacked = jnp.kron(jnp.eye(TILE // nodes_per_cell, dtype=BF), kinetic.T)
    inv_root = inv_mass_root[None]
    potential = potential[None]
    boundary = boundary[None]
    width = boundary.shape[1]

    scaled, rim = pl.pallas_call(
        prepare_kernel,
        out_shape=(
            jax.ShapeDtypeStruct((rows, owned), BF),
            jax.ShapeDtypeStruct((rows, width), BF),
        ),
        name="prepare",
    )(states_in, inv_root, boundary)
    own, ghost = cells(scaled, exchange_out(rim), index, scale, stacked)
    first, scaled, rim = pl.pallas_call(
        first_kernel,
        out_shape=(
            jax.ShapeDtypeStruct((rows, owned), BF),
            jax.ShapeDtypeStruct((rows, owned), BF),
            jax.ShapeDtypeStruct((rows, width), BF),
        ),
        name="first",
    )(own, exchange_back(ghost), scaled, states_in, inv_root, potential, boundary)
    own, ghost = cells(scaled, exchange_out(rim), index, scale, stacked)
    filtered = pl.pallas_call(
        second_kernel,
        out_shape=jax.ShapeDtypeStruct((rows, owned), BF),
        name="second",
    )(own, exchange_back(ghost), scaled, states_in, first, inv_root, potential, boundary)

    bands = lax.axis_size("band")
    outer = lax.axis_size(SPACE[0])
    node_total = owned * outer * QUAD
    regrouped = lax.all_to_all(filtered, "band", split_axis=1, concat_axis=0, tiled=True)
    partial_sum = lax.dot_general(regrouped, regrouped, (((1,), (1,)), ((), ())), preferred_element_type=F32)
    states = partial_sum.shape[0]
    blocks = partial_sum.astype(BF).reshape(bands * QUAD, states // (bands * QUAD), states)
    sums = lax.all_to_all(blocks, ("band", SPACE[1]), 0, 0, tiled=True).astype(F32).sum(axis=0)
    spread = jnp.broadcast_to(sums.astype(BF)[None], (outer, *sums.shape))
    total = lax.all_to_all(spread, SPACE[0], 0, 0, tiled=True).astype(F32).sum(axis=0)
    margin = lax.all_gather(total / node_total, SPACE[1], axis=0, tiled=True)
    return filtered, margin


def solution(mesh):
    bands = mesh.shape["band"]
    split = Mesh(mesh.devices.reshape(-1, QUAD, bands), (*SPACE, "band"))
    in_specs = (P("band", SPACE), P(), P(SPACE), P(None, SPACE), P(SPACE), P(SPACE), P(SPACE))
    out_specs = (P("band", SPACE), P("band", None))
    return jax.shard_map(body, mesh=split, in_specs=in_specs, out_specs=out_specs, check_vma=False)
```

```python
import jax
import jax.numpy as jnp
from jax import lax
from jax.experimental import pallas as pl
from jax.experimental.pallas import tpu as pltpu
from jax.sharding import Mesh
from jax.sharding import PartitionSpec as P

SPACE = ("outer", "quad")
QUAD = 4
OFFSETS = (-2, -1, 1, 2)
CENTER = 0.5
HALF = 6.0
TILE = 256
STEP = 2048
BF = jnp.bfloat16
F32 = jnp.float32


def selection(low, count):
    width = low.shape[1]
    lines = lax.broadcasted_iota(jnp.int32, (TILE, width), 0).astype(F32).astype(BF)
    place = (low % TILE).astype(F32)
    tiles = []
    for tile in range(count // TILE):
        here = jnp.where(low // TILE == tile, place, -1.0).astype(BF)
        tiles.append(jnp.where(lines == here, jnp.ones((), BF), jnp.zeros((), BF)))
    return jnp.concatenate(tiles, axis=0)


def picked(values, chosen):
    return jnp.dot(values, chosen, preferred_element_type=F32)


def put_back(values, chosen):
    return lax.dot_general(values, chosen, (((1,), (1,)), ((), ())), preferred_element_type=F32)


def from_pieces(values, piece, count):
    return jnp.concatenate([values[:, i * piece : (i + 1) * piece] for i in range(count)], axis=0)


def take_columns(values, index, piece):
    rows, count = values.shape[0], values.shape[1] // piece
    both = picked(from_pieces(values, piece, count), selection(index % piece, piece))
    part = index // piece
    result = both[:rows]
    for i in range(1, count):
        result = jnp.where(part == i, both[i * rows : (i + 1) * rows], result)
    return result


def add_columns(values, index, piece, count):
    rows = values.shape[0]
    part = index // piece
    none = jnp.zeros((), values.dtype)
    spread = jnp.concatenate([jnp.where(part == i, values, none) for i in range(count)], axis=0)
    sums = put_back(spread, selection(index % piece, piece))
    return [sums[i * rows : (i + 1) * rows] for i in range(count)]


def prepare_kernel(values, inv_root, boundary, scaled_ref, rim_ref):
    scaled = (inv_root[...] * values[...].astype(F32)).astype(BF)
    scaled_ref[...] = scaled
    rim_ref[...] = take_columns(scaled, boundary[...], boundary.shape[1]).astype(BF)


def cells_kernel(mine, index, scale, kinetic, scaled, near, far, farther, own_ref, near_ref, far_ref, farther_ref, table, acc):
    step = pl.program_id(0)
    place = mine[0]
    rows, piece = far.shape
    own_count = scaled.shape[1] // piece
    count = own_count + len(OFFSETS)

    @pl.when(step == 0)
    def _():
        for i in range(own_count):
            table[i * rows : (i + 1) * rows] = scaled[:, i * piece : (i + 1) * piece]
        for i, offset in enumerate(OFFSETS):
            low = (own_count + i) * rows
            member = place + offset
            inside = jnp.logical_and(member >= 0, member < QUAD)

            @pl.when(inside)
            def _():
                table[low : low + rows] = near[jnp.clip(member, 0, QUAD - 1)]

            @pl.when(jnp.logical_not(inside))
            def _():
                table[low : low + rows] = (far if abs(offset) == 2 else farther)[...]

    places = index[...]
    chosen = selection(places % piece, piece)
    part = places // piece
    both = picked(table[...], chosen)
    gathered = both[:rows]
    for i in range(1, count):
        gathered = jnp.where(part == i, both[i * rows : (i + 1) * rows], gathered)
    gathered = gathered.astype(BF)
    terms = jnp.concatenate(
        [picked(gathered[:, i : i + TILE], kinetic[...]) for i in range(0, STEP, TILE)], axis=1
    )
    terms = terms * scale[...]
    spread = jnp.concatenate([jnp.where(part == i, terms, 0.0).astype(BF) for i in range(count)], axis=0)
    sums = put_back(spread, chosen)

    @pl.when(step == 0)
    def _():
        acc[...] = sums

    @pl.when(step > 0)
    def _():
        acc[...] += sums

    @pl.when(step == pl.num_programs(0) - 1)
    def _():
        def slot(i):
            return acc[(own_count + i) * rows : (own_count + i + 1) * rows].astype(BF)

        for i in range(own_count):
            own_ref[:, i * piece : (i + 1) * piece] = acc[i * rows : (i + 1) * rows]
        near_ref[...] = jnp.zeros_like(near_ref)
        for i, offset in enumerate(OFFSETS):
            member = place + offset

            @pl.when(jnp.logical_and(member >= 0, member < QUAD))
            def _():
                near_ref[jnp.clip(member, 0, QUAD - 1)] = slot(i)

        @pl.when(place < 2)
        def _():
            far_ref[...] = slot(0)
            farther_ref[...] = slot(1)

        @pl.when(place >= 2)
        def _():
            far_ref[...] = slot(3)
            farther_ref[...] = slot(2)


def cells(mine, scaled, ghosts, index, scale, kinetic):
    rows, owned = scaled.shape
    near, far, _ = ghosts
    piece = far.shape[1]
    places = index.shape[1]
    line = pl.BlockSpec((1, STEP), lambda i, mine: (0, i))

    def whole(shape):
        return pl.BlockSpec(shape, lambda i, mine: (0,) * len(shape))

    stack = (owned // piece + len(OFFSETS)) * rows
    blocks = [whole(near.shape), whole(far.shape), whole(far.shape)]
    own, *ghosts = pl.pallas_call(
        cells_kernel,
        grid_spec=pltpu.PrefetchScalarGridSpec(
            num_scalar_prefetch=1,
            grid=(places // STEP,),
            in_specs=[line, line, whole(kinetic.shape), whole(scaled.shape), *blocks],
            out_specs=[whole(scaled.shape), *blocks],
            scratch_shapes=[pltpu.VMEM((stack, piece), BF), pltpu.VMEM((stack, piece), F32)],
        ),
        out_shape=(
            jax.ShapeDtypeStruct((rows, owned), F32),
            jax.ShapeDtypeStruct(near.shape, BF),
            jax.ShapeDtypeStruct(far.shape, BF),
            jax.ShapeDtypeStruct(far.shape, BF),
        ),
        name="cells",
    )(mine, index, scale, kinetic, scaled, *ghosts)
    return own, ghosts


def image_of(own, near, far, farther, scaled, inv_root, potential, boundary):
    back = far[...].astype(F32) + farther[...].astype(F32)
    for i in range(QUAD):
        back = back + near[i].astype(F32)
    upper = back.astype(BF)
    lower = (back - upper.astype(F32)).astype(BF)
    rows, piece = back.shape
    sums = add_columns(jnp.concatenate([upper, lower], axis=0), boundary[...], piece, own.shape[1] // piece)
    total = own[...] + jnp.concatenate([part[:rows] + part[rows:] for part in sums], axis=1)
    return inv_root[...] * (total + potential[...] * scaled[...].astype(F32))


def first_kernel(own, near, far, farther, scaled, start, inv_root, potential, boundary, first_ref, scaled_ref, rim_ref):
    image = image_of(own, near, far, farther, scaled, inv_root, potential, boundary)
    first = ((image - CENTER * start[...].astype(F32)) / HALF).astype(BF)
    first_ref[...] = first
    scaled_new = (inv_root[...] * first.astype(F32)).astype(BF)
    scaled_ref[...] = scaled_new
    rim_ref[...] = take_columns(scaled_new, boundary[...], boundary.shape[1]).astype(BF)


def second_kernel(own, near, far, farther, scaled, start, first, inv_root, potential, boundary, out_ref, block_ref):
    image = image_of(own, near, far, farther, scaled, inv_root, potential, boundary)
    second = 2.0 * (image - CENTER * first[...].astype(F32)) / HALF - start[...].astype(F32)
    second = second.astype(BF)
    out_ref[...] = second
    width = block_ref.shape[2]
    for i in range(block_ref.shape[0]):
        block_ref[i] = second[:, i * width : (i + 1) * width]


def swapped(x, pairs):
    quads = lax.axis_size(SPACE[0])
    sends = []
    for m in range(quads):
        for here, there in pairs.items():
            ends = (m * QUAD + here, (m + 1) % quads * QUAD + there)
            sends += [ends, ends[::-1]]
    return lax.ppermute(x, SPACE, sends)


def both_across(far, farther):
    return swapped(far, {2: 0, 3: 1}), swapped(farther, {3: 0})


def exchange_out(rim):
    far, farther = both_across(rim, rim)
    return lax.all_gather(rim, SPACE[1], axis=0), far, farther


def exchange_back(near, far, farther):
    far, farther = both_across(far, farther)
    return lax.all_to_all(near, SPACE[1], 0, 0, tiled=True), far, farther


def body(states_in, kinetic, cell_scale, cell_nodes, boundary, potential, inv_mass_root):
    nodes_per_cell = kinetic.shape[0]
    rows, owned = states_in.shape
    index = cell_nodes.T.reshape(1, -1)
    scale = jnp.repeat(cell_scale, nodes_per_cell).reshape(1, -1)
    stacked = jnp.kron(jnp.eye(TILE // nodes_per_cell, dtype=BF), kinetic.T)
    inv_root = inv_mass_root[None]
    potential = potential[None]
    boundary = boundary[None]
    width = boundary.shape[1]
    bands = lax.axis_size("band")
    mine = lax.axis_index(SPACE[1])[None]

    scaled, rim = pl.pallas_call(
        prepare_kernel,
        out_shape=(
            jax.ShapeDtypeStruct((rows, owned), BF),
            jax.ShapeDtypeStruct((rows, width), BF),
        ),
        name="prepare",
    )(states_in, inv_root, boundary)
    own, ghost = cells(mine, scaled, exchange_out(rim), index, scale, stacked)
    first, scaled, rim = pl.pallas_call(
        first_kernel,
        out_shape=(
            jax.ShapeDtypeStruct((rows, owned), BF),
            jax.ShapeDtypeStruct((rows, owned), BF),
            jax.ShapeDtypeStruct((rows, width), BF),
        ),
        name="first",
    )(own, *exchange_back(*ghost), scaled, states_in, inv_root, potential, boundary)
    own, ghost = cells(mine, scaled, exchange_out(rim), index, scale, stacked)
    filtered, blocks = pl.pallas_call(
        second_kernel,
        out_shape=(
            jax.ShapeDtypeStruct((rows, owned), BF),
            jax.ShapeDtypeStruct((bands, rows, owned // bands), BF),
        ),
        name="second",
    )(own, *exchange_back(*ghost), scaled, states_in, first, inv_root, potential, boundary)

    outer = lax.axis_size(SPACE[0])
    node_total = owned * outer * QUAD
    regrouped = lax.all_to_all(blocks, "band", 0, 0, tiled=True).reshape(bands * rows, -1)
    partial_sum = lax.dot_general(regrouped, regrouped, (((1,), (1,)), ((), ())), preferred_element_type=F32)
    states = partial_sum.shape[0]
    blocks = partial_sum.astype(BF).reshape(bands * QUAD, states // (bands * QUAD), states)
    sums = lax.all_to_all(blocks, ("band", SPACE[1]), 0, 0, tiled=True).astype(F32).sum(axis=0)
    spread = jnp.broadcast_to(sums.astype(BF)[None], (outer, *sums.shape))
    total = lax.all_to_all(spread, SPACE[0], 0, 0, tiled=True).astype(F32).sum(axis=0)
    margin = lax.all_gather(total / node_total, SPACE[1], axis=0, tiled=True)
    return filtered, margin


def solution(mesh):
    bands = mesh.shape["band"]
    split = Mesh(mesh.devices.reshape(-1, QUAD, bands), (*SPACE, "band"))
    in_specs = (P("band", SPACE), P(), P(SPACE), P(None, SPACE), P(SPACE), P(SPACE), P(SPACE))
    out_specs = (P("band", SPACE), P("band", None))
    return jax.shard_map(body, mesh=split, in_specs=in_specs, out_specs=out_specs, check_vma=False)
```

```python
import jax
import jax.numpy as jnp
from jax import lax
from jax.experimental import pallas as pl
from jax.experimental.pallas import tpu as pltpu
from jax.sharding import Mesh
from jax.sharding import PartitionSpec as P

SPACE = ("outer", "quad")
QUAD = 4
OFFSETS = (-2, -1, 1, 2)
CENTER = 0.5
HALF = 6.0
TILE = 256
STEP = 2048
BF = jnp.bfloat16
F32 = jnp.float32


def selection(low, count):
    width = low.shape[1]
    lines = lax.broadcasted_iota(jnp.int32, (TILE, width), 0).astype(F32).astype(BF)
    place = (low % TILE).astype(F32)
    tiles = []
    for tile in range(count // TILE):
        here = jnp.where(low // TILE == tile, place, -1.0).astype(BF)
        tiles.append(jnp.where(lines == here, jnp.ones((), BF), jnp.zeros((), BF)))
    return jnp.concatenate(tiles, axis=0)


def picked(values, chosen):
    return jnp.dot(values, chosen, preferred_element_type=F32)


def put_back(values, chosen):
    return lax.dot_general(values, chosen, (((1,), (1,)), ((), ())), preferred_element_type=F32)


def from_pieces(values, piece, count):
    return jnp.concatenate([values[:, i * piece : (i + 1) * piece] for i in range(count)], axis=0)


def take_columns(values, index, piece):
    rows, count = values.shape[0], values.shape[1] // piece
    both = picked(from_pieces(values, piece, count), selection(index % piece, piece))
    part = index // piece
    result = both[:rows]
    for i in range(1, count):
        result = jnp.where(part == i, both[i * rows : (i + 1) * rows], result)
    return result


def add_columns(values, index, piece, count):
    rows = values.shape[0]
    part = index // piece
    none = jnp.zeros((), values.dtype)
    spread = jnp.concatenate([jnp.where(part == i, values, none) for i in range(count)], axis=0)
    sums = put_back(spread, selection(index % piece, piece))
    return [sums[i * rows : (i + 1) * rows] for i in range(count)]


def prepare_kernel(values, inv_root, boundary, scaled_ref, rim_ref):
    scaled = (inv_root[...] * values[...].astype(F32)).astype(BF)
    scaled_ref[...] = scaled
    rim_ref[...] = take_columns(scaled, boundary[...], boundary.shape[1]).astype(BF)


def slot(odd, i):
    return jnp.where(odd == 1, len(OFFSETS) - 1 - i, i)


def own_gather_kernel(index, scaled, out_ref, table):
    rows = scaled.shape[0]
    count, piece = table.shape[0] // rows, table.shape[1]

    @pl.when(pl.program_id(0) == 0)
    def _():
        table[...] = from_pieces(scaled[...], piece, count)

    places = index[...]
    part = places // piece
    both = picked(table[...], selection(places % piece, piece))
    gathered = jnp.zeros((), F32)
    for i in range(count):
        gathered = jnp.where(part == i, both[i * rows : (i + 1) * rows], gathered)
    out_ref[...] = gathered.astype(BF)


def own_gather(scaled, index, piece):
    rows, owned = scaled.shape
    places = index.shape[1]
    return pl.pallas_call(
        own_gather_kernel,
        grid=(places // STEP,),
        in_specs=[
            pl.BlockSpec((1, STEP), lambda i: (0, i)),
            pl.BlockSpec(scaled.shape, lambda i: (0, 0)),
        ],
        out_specs=pl.BlockSpec((rows, STEP), lambda i: (0, i)),
        out_shape=jax.ShapeDtypeStruct((rows, places), BF),
        scratch_shapes=[pltpu.VMEM((owned // piece * rows, piece), BF)],
        name="own_gather",
    )(index, scaled)


def cells_kernel(first, odd, index, scale, kinetic, own, across, partner, past, term_ref, send_ref, keep_ref, table, acc):
    step = pl.program_id(0)
    rows, piece = partner.shape
    count = len(OFFSETS)

    @pl.when(step == 0)
    def _():
        for i, side in enumerate((across[1], across[0], partner[...], past[...])):
            low = pl.multiple_of(slot(odd[0], i) * rows, rows)
            table[pl.ds(low, rows)] = side

    places = index[...]
    chosen = selection(places % piece, piece)
    part = places // piece - first
    both = picked(table[...], chosen)
    gathered = own[...].astype(F32)
    for i in range(count):
        gathered = jnp.where(part == i, both[i * rows : (i + 1) * rows], gathered)
    gathered = gathered.astype(BF)
    terms = jnp.concatenate(
        [picked(gathered[:, i : i + TILE], kinetic[...]) for i in range(0, STEP, TILE)], axis=1
    )
    terms = terms * scale[...]
    term_ref[...] = terms.astype(BF)
    spread = jnp.concatenate([jnp.where(part == i, terms, 0.0).astype(BF) for i in range(count)], axis=0)
    sums = put_back(spread, chosen)

    @pl.when(step == 0)
    def _():
        acc[...] = sums

    @pl.when(step > 0)
    def _():
        acc[...] += sums

    @pl.when(step == pl.num_programs(0) - 1)
    def _():
        def side(i):
            low = pl.multiple_of(slot(odd[0], i) * rows, rows)
            return acc[pl.ds(low, rows)].astype(BF)

        send_ref[0] = side(3)
        send_ref[1] = side(2)
        keep_ref[0] = side(0)
        keep_ref[1] = side(1)


def cells(odd, own, across, partner, past, index, scale, kinetic, owned):
    rows, piece = partner.shape
    places = index.shape[1]
    count = len(OFFSETS)

    def kernel(*refs):
        cells_kernel(owned // piece, *refs)

    line = pl.BlockSpec((1, STEP), lambda i, odd: (0, i))
    wide = pl.BlockSpec((rows, STEP), lambda i, odd: (0, i))

    def whole(shape):
        return pl.BlockSpec(shape, lambda i, odd: (0,) * len(shape))

    pair = (2, rows, piece)
    return pl.pallas_call(
        kernel,
        grid_spec=pltpu.PrefetchScalarGridSpec(
            num_scalar_prefetch=1,
            grid=(places // STEP,),
            in_specs=[line, line, whole(kinetic.shape), wide, whole(pair), whole(partner.shape), whole(partner.shape)],
            out_specs=[wide, whole(pair), whole(pair)],
            scratch_shapes=[pltpu.VMEM((count * rows, piece), BF), pltpu.VMEM((count * rows, piece), F32)],
        ),
        out_shape=(
            jax.ShapeDtypeStruct((rows, places), BF),
            jax.ShapeDtypeStruct(pair, BF),
            jax.ShapeDtypeStruct(pair, BF),
        ),
        name="cells",
    )(odd, index, scale, kinetic, own, across, partner, past)


def own_sum_kernel(index, terms, out_ref, acc):
    step = pl.program_id(0)
    rows = terms.shape[0]
    piece = acc.shape[1]
    count = acc.shape[0] // rows
    places = index[...]
    part = places // piece
    values = terms[...].astype(F32)
    spread = jnp.concatenate([jnp.where(part == i, values, 0.0).astype(BF) for i in range(count)], axis=0)
    sums = put_back(spread, selection(places % piece, piece))

    @pl.when(step == 0)
    def _():
        acc[...] = sums

    @pl.when(step > 0)
    def _():
        acc[...] += sums

    @pl.when(step == pl.num_programs(0) - 1)
    def _():
        for i in range(count):
            out_ref[:, i * piece : (i + 1) * piece] = acc[i * rows : (i + 1) * rows]


def own_sum(terms, index, owned, piece):
    rows, places = terms.shape
    return pl.pallas_call(
        own_sum_kernel,
        grid=(places // STEP,),
        in_specs=[
            pl.BlockSpec((1, STEP), lambda i: (0, i)),
            pl.BlockSpec((rows, STEP), lambda i: (0, i)),
        ],
        out_specs=pl.BlockSpec((rows, owned), lambda i: (0, 0)),
        out_shape=jax.ShapeDtypeStruct((rows, owned), F32),
        scratch_shapes=[pltpu.VMEM((owned // piece * rows, piece), F32)],
        name="own_sum",
    )(index, terms)


def image_of(own, partner, across, past, scaled, inv_root, potential, boundary):
    back = partner[1].astype(F32) + across[1].astype(F32) + past[...].astype(F32)
    upper = back.astype(BF)
    lower = (back - upper.astype(F32)).astype(BF)
    rows, piece = back.shape
    sums = add_columns(jnp.concatenate([upper, lower], axis=0), boundary[...], piece, own.shape[1] // piece)
    total = own[...] + jnp.concatenate([part[:rows] + part[rows:] for part in sums], axis=1)
    return inv_root[...] * (total + potential[...] * scaled[...].astype(F32))


def first_kernel(own, partner, across, past, scaled, start, inv_root, potential, boundary, first_ref, scaled_ref, rim_ref):
    image = image_of(own, partner, across, past, scaled, inv_root, potential, boundary)
    first = ((image - CENTER * start[...].astype(F32)) / HALF).astype(BF)
    first_ref[...] = first
    scaled_new = (inv_root[...] * first.astype(F32)).astype(BF)
    scaled_ref[...] = scaled_new
    rim_ref[...] = take_columns(scaled_new, boundary[...], boundary.shape[1]).astype(BF)


def second_kernel(own, partner, across, past, scaled, start, first, inv_root, potential, boundary, out_ref, block_ref):
    image = image_of(own, partner, across, past, scaled, inv_root, potential, boundary)
    second = 2.0 * (image - CENTER * first[...].astype(F32)) / HALF - start[...].astype(F32)
    second = second.astype(BF)
    out_ref[...] = second
    width = block_ref.shape[2]
    for i in range(block_ref.shape[0]):
        block_ref[i] = second[:, i * width : (i + 1) * width]


def with_core(x):
    count = QUAD * lax.axis_size(SPACE[0])
    return lax.ppermute(x, SPACE, [(i, i ^ 1) for i in range(count)])


def with_chip(x):
    count = QUAD * lax.axis_size(SPACE[0])
    return lax.ppermute(x, SPACE, [(i, (i + 2 * (i % 2) - 1) % count) for i in range(count)])


def body(states_in, kinetic, cell_scale, cell_nodes, boundary, potential, inv_mass_root):
    nodes_per_cell = kinetic.shape[0]
    rows, owned = states_in.shape
    index = cell_nodes.T.reshape(1, -1)
    scale = jnp.repeat(cell_scale, nodes_per_cell).reshape(1, -1)
    stacked = jnp.kron(jnp.eye(TILE // nodes_per_cell, dtype=BF), kinetic.T)
    inv_root = inv_mass_root[None]
    potential = potential[None]
    boundary = boundary[None]
    width = boundary.shape[1]
    bands = lax.axis_size("band")
    odd = (lax.axis_index(SPACE[1]) % 2)[None]

    scaled, rim = pl.pallas_call(
        prepare_kernel,
        out_shape=(
            jax.ShapeDtypeStruct((rows, owned), BF),
            jax.ShapeDtypeStruct((rows, width), BF),
        ),
        name="prepare",
    )(states_in, inv_root, boundary)

    def operate(scaled, rim):
        partner = with_core(rim)
        across = with_chip(jnp.stack([rim, partner]))
        held, _ = lax.optimization_barrier((scaled, partner))
        edge, own = lax.optimization_barrier((across[0], own_gather(held, index, width)))
        past = with_core(edge)
        terms, send, keep = cells(odd, own, across, partner, past, index, scale, stacked, owned)
        partner = with_core(send)
        across = with_chip(jnp.stack([keep[0], (keep[1].astype(F32) + partner[0].astype(F32)).astype(BF)]))
        held, _ = lax.optimization_barrier((terms, partner))
        edge, own = lax.optimization_barrier((across[0], own_sum(held, index, owned, width)))
        past = with_core(edge)
        return own, partner, across, past

    arrived = operate(scaled, rim)
    first, scaled_first, rim = pl.pallas_call(
        first_kernel,
        out_shape=(
            jax.ShapeDtypeStruct((rows, owned), BF),
            jax.ShapeDtypeStruct((rows, owned), BF),
            jax.ShapeDtypeStruct((rows, width), BF),
        ),
        name="first",
    )(*arrived, scaled, states_in, inv_root, potential, boundary)
    arrived = operate(scaled_first, rim)
    filtered, blocks = pl.pallas_call(
        second_kernel,
        out_shape=(
            jax.ShapeDtypeStruct((rows, owned), BF),
            jax.ShapeDtypeStruct((bands, rows, owned // bands), BF),
        ),
        name="second",
    )(*arrived, scaled_first, states_in, first, inv_root, potential, boundary)

    outer = lax.axis_size(SPACE[0])
    node_total = owned * outer * QUAD
    regrouped = lax.all_to_all(blocks, "band", 0, 0, tiled=True).reshape(bands * rows, -1)
    partial_sum = lax.dot_general(regrouped, regrouped, (((1,), (1,)), ((), ())), preferred_element_type=F32)
    states = partial_sum.shape[0]
    blocks = partial_sum.astype(BF).reshape(bands * QUAD, states // (bands * QUAD), states)
    sums = lax.all_to_all(blocks, ("band", SPACE[1]), 0, 0, tiled=True).astype(F32).sum(axis=0)
    spread = jnp.broadcast_to(sums.astype(BF)[None], (outer, *sums.shape))
    total = lax.all_to_all(spread, SPACE[0], 0, 0, tiled=True).astype(F32).sum(axis=0)
    margin = lax.all_gather(total / node_total, SPACE[1], axis=0, tiled=True)
    return filtered, margin


def solution(mesh):
    bands = mesh.shape["band"]
    split = Mesh(mesh.devices.reshape(-1, QUAD, bands), (*SPACE, "band"))
    in_specs = (P("band", SPACE), P(), P(SPACE), P(None, SPACE), P(SPACE), P(SPACE), P(SPACE))
    out_specs = (P("band", SPACE), P("band", None))
    return jax.shard_map(body, mesh=split, in_specs=in_specs, out_specs=out_specs, check_vma=False)
```

```python
import jax
import jax.numpy as jnp
from jax import lax
from jax.experimental import pallas as pl
from jax.experimental.pallas import tpu as pltpu
from jax.sharding import Mesh
from jax.sharding import PartitionSpec as P

SPACE = ("outer", "quad")
QUAD = 4
OFFSETS = (-2, -1, 1, 2)
CENTER = 0.5
HALF = 6.0
TILE = 256
STEP = 2048
OWN_STEP = 4096
ROOM = 24 * 2**20
BF = jnp.bfloat16
F32 = jnp.float32


def selection(low, count):
    width = low.shape[1]
    lines = lax.broadcasted_iota(jnp.int32, (TILE, width), 0).astype(F32).astype(BF)
    place = (low % TILE).astype(F32)
    tiles = []
    for tile in range(count // TILE):
        here = jnp.where(low // TILE == tile, place, -1.0).astype(BF)
        tiles.append(jnp.where(lines == here, jnp.ones((), BF), jnp.zeros((), BF)))
    return jnp.concatenate(tiles, axis=0)


def picked(values, chosen):
    return jnp.dot(values, chosen, preferred_element_type=F32)


def put_back(values, chosen):
    return lax.dot_general(values, chosen, (((1,), (1,)), ((), ())), preferred_element_type=F32)


def from_pieces(values, piece, count):
    return jnp.concatenate([values[:, i * piece : (i + 1) * piece] for i in range(count)], axis=0)


def take_columns(values, index, piece):
    rows, count = values.shape[0], values.shape[1] // piece
    both = picked(from_pieces(values, piece, count), selection(index % piece, piece))
    part = index // piece
    result = both[:rows]
    for i in range(1, count):
        result = jnp.where(part == i, both[i * rows : (i + 1) * rows], result)
    return result


def add_columns(values, index, piece, count):
    rows = values.shape[0]
    part = index // piece
    none = jnp.zeros((), values.dtype)
    spread = jnp.concatenate([jnp.where(part == i, values, none) for i in range(count)], axis=0)
    sums = put_back(spread, selection(index % piece, piece))
    return [sums[i * rows : (i + 1) * rows] for i in range(count)]


def prepare_kernel(values, inv_root, boundary, scaled_ref, rim_ref):
    scaled = (inv_root[...] * values[...].astype(F32)).astype(BF)
    scaled_ref[...] = scaled
    rim_ref[...] = take_columns(scaled, boundary[...], boundary.shape[1]).astype(BF)


def slot(odd, i):
    return jnp.where(odd == 1, len(OFFSETS) - 1 - i, i)


def own_gather_kernel(index, scaled, out_ref, table):
    rows = scaled.shape[0]
    count, piece = table.shape[0] // rows, table.shape[1]

    @pl.when(pl.program_id(0) == 0)
    def _():
        table[...] = from_pieces(scaled[...], piece, count)

    places = index[...]
    part = places // piece
    both = picked(table[...], selection(places % piece, piece))
    gathered = jnp.zeros((), F32)
    for i in range(count):
        gathered = jnp.where(part == i, both[i * rows : (i + 1) * rows], gathered)
    out_ref[...] = gathered.astype(BF)


def own_gather(scaled, index, piece):
    rows, owned = scaled.shape
    places = index.shape[1]
    return pl.pallas_call(
        own_gather_kernel,
        grid=(places // OWN_STEP,),
        in_specs=[
            pl.BlockSpec((1, OWN_STEP), lambda i: (0, i)),
            pl.BlockSpec(scaled.shape, lambda i: (0, 0)),
        ],
        out_specs=pl.BlockSpec((rows, OWN_STEP), lambda i: (0, i)),
        out_shape=jax.ShapeDtypeStruct((rows, places), BF),
        scratch_shapes=[pltpu.VMEM((owned // piece * rows, piece), BF)],
        name="own_gather",
        compiler_params=pltpu.CompilerParams(vmem_limit_bytes=ROOM),
    )(index, scaled)


def cells_kernel(first, odd, index, scale, kinetic, own, across, chip, past, term_ref, send_ref, keep_ref, table, matrix, acc):
    step = pl.program_id(0)
    _, rows, piece = chip.shape
    count = len(OFFSETS)

    @pl.when(step == 0)
    def _():
        @pl.when(odd[0] == 0)
        def _():
            for i, ghosts in enumerate((across[0], across[1], chip[1], past[0])):
                table[i * rows : (i + 1) * rows] = ghosts

        @pl.when(odd[0] == 1)
        def _():
            for i, ghosts in enumerate((past[1], chip[0], across[0], across[1])):
                table[i * rows : (i + 1) * rows] = ghosts

        matrix[...] = jnp.zeros_like(matrix)
        nodes = kinetic.shape[0]
        for i in range(TILE // nodes):
            matrix[i * nodes : (i + 1) * nodes, i * nodes : (i + 1) * nodes] = kinetic[...]

    places = index[...]
    chosen = selection(places % piece, piece)
    part = places // piece - first
    both = picked(table[...], chosen)
    gathered = own[...].astype(F32)
    for i in range(count):
        gathered = jnp.where(part == i, both[i * rows : (i + 1) * rows], gathered)
    gathered = gathered.astype(BF)
    terms = jnp.concatenate(
        [put_back(gathered[:, i : i + TILE], matrix[...]) for i in range(0, STEP, TILE)], axis=1
    )
    terms = terms * scale[...]
    term_ref[...] = terms.astype(BF)
    spread = jnp.concatenate([jnp.where(part == i, terms, 0.0).astype(BF) for i in range(count)], axis=0)
    sums = put_back(spread, chosen)

    @pl.when(step == 0)
    def _():
        acc[...] = sums

    @pl.when(step > 0)
    def _():
        acc[...] += sums

    @pl.when(step == pl.num_programs(0) - 1)
    def _():
        def side(i):
            low = pl.multiple_of(slot(odd[0], i) * rows, rows)
            return acc[pl.ds(low, rows)].astype(BF)

        send_ref[0] = jnp.zeros((rows, piece), BF)
        send_ref[1] = side(3)
        send_ref[2] = side(2)
        keep_ref[0] = side(0)
        keep_ref[1] = side(1)


def cells(odd, own, across, chip, past, index, scale, kinetic, owned):
    _, rows, piece = chip.shape
    places = index.shape[1]
    count = len(OFFSETS)

    def kernel(*refs):
        cells_kernel(owned // piece, *refs)

    line = pl.BlockSpec((1, STEP), lambda i, odd: (0, i))
    wide = pl.BlockSpec((rows, STEP), lambda i, odd: (0, i))

    def whole(shape):
        return pl.BlockSpec(shape, lambda i, odd: (0,) * len(shape))

    pair, triple = (2, rows, piece), (3, rows, piece)
    return pl.pallas_call(
        kernel,
        grid_spec=pltpu.PrefetchScalarGridSpec(
            num_scalar_prefetch=1,
            grid=(places // STEP,),
            in_specs=[line, line, whole(kinetic.shape), wide, whole(pair), whole(pair), whole(pair)],
            out_specs=[wide, whole(triple), whole(pair)],
            scratch_shapes=[pltpu.VMEM((count * rows, piece), BF), pltpu.VMEM((TILE, TILE), BF), pltpu.VMEM((count * rows, piece), F32)],
        ),
        out_shape=(
            jax.ShapeDtypeStruct((rows, places), BF),
            jax.ShapeDtypeStruct(triple, BF),
            jax.ShapeDtypeStruct(pair, BF),
        ),
        name="cells",
        compiler_params=pltpu.CompilerParams(vmem_limit_bytes=ROOM),
    )(odd, index, scale, kinetic, own, across, chip, past)


def own_sum_kernel(index, terms, out_ref, acc):
    step = pl.program_id(0)
    rows = terms.shape[0]
    piece = acc.shape[1]
    count = acc.shape[0] // rows
    places = index[...]
    part = places // piece
    values = terms[...].astype(F32)
    spread = jnp.concatenate([jnp.where(part == i, values, 0.0).astype(BF) for i in range(count)], axis=0)
    sums = put_back(spread, selection(places % piece, piece))

    @pl.when(step == 0)
    def _():
        acc[...] = sums

    @pl.when(step > 0)
    def _():
        acc[...] += sums

    @pl.when(step == pl.num_programs(0) - 1)
    def _():
        for i in range(count):
            out_ref[:, i * piece : (i + 1) * piece] = acc[i * rows : (i + 1) * rows]


def own_sum(terms, index, owned, piece):
    rows, places = terms.shape
    return pl.pallas_call(
        own_sum_kernel,
        grid=(places // OWN_STEP,),
        in_specs=[
            pl.BlockSpec((1, OWN_STEP), lambda i: (0, i)),
            pl.BlockSpec((rows, OWN_STEP), lambda i: (0, i)),
        ],
        out_specs=pl.BlockSpec((rows, owned), lambda i: (0, 0)),
        out_shape=jax.ShapeDtypeStruct((rows, owned), F32),
        scratch_shapes=[pltpu.VMEM((owned // piece * rows, piece), F32)],
        name="own_sum",
        compiler_params=pltpu.CompilerParams(vmem_limit_bytes=ROOM),
    )(index, terms)


def image_of(own, partner, across, past, scaled, inv_root, potential, boundary):
    back = partner[2].astype(F32) + across[1].astype(F32) + past[...].astype(F32)
    upper = back.astype(BF)
    lower = (back - upper.astype(F32)).astype(BF)
    rows, piece = back.shape
    sums = add_columns(jnp.concatenate([upper, lower], axis=0), boundary[...], piece, own.shape[1] // piece)
    total = own[...] + jnp.concatenate([part[:rows] + part[rows:] for part in sums], axis=1)
    return inv_root[...] * (total + potential[...] * scaled[...].astype(F32))


def first_kernel(own, partner, across, past, scaled, start, inv_root, potential, boundary, first_ref, scaled_ref, rim_ref):
    image = image_of(own, partner, across, past, scaled, inv_root, potential, boundary)
    first = ((image - CENTER * start[...].astype(F32)) / HALF).astype(BF)
    first_ref[...] = first
    scaled_new = (inv_root[...] * first.astype(F32)).astype(BF)
    scaled_ref[...] = scaled_new
    rim_ref[...] = take_columns(scaled_new, boundary[...], boundary.shape[1]).astype(BF)


def second_kernel(own, partner, across, past, scaled, start, first, inv_root, potential, boundary, out_ref, block_ref):
    image = image_of(own, partner, across, past, scaled, inv_root, potential, boundary)
    second = 2.0 * (image - CENTER * first[...].astype(F32)) / HALF - start[...].astype(F32)
    second = second.astype(BF)
    out_ref[...] = second
    width = block_ref.shape[2]
    for i in range(block_ref.shape[0]):
        block_ref[i] = second[:, i * width : (i + 1) * width]


def with_core(x):
    count = QUAD * lax.axis_size(SPACE[0])
    return lax.ppermute(x, SPACE, [(i, i ^ 1) for i in range(count)])


def with_chip(x):
    count = QUAD * lax.axis_size(SPACE[0])
    return lax.ppermute(x, SPACE, [(i, (i + 2 * (i % 2) - 1) % count) for i in range(count)])


def body(states_in, kinetic, cell_scale, cell_nodes, boundary, potential, inv_mass_root):
    nodes_per_cell = kinetic.shape[0]
    rows, owned = states_in.shape
    index = cell_nodes.T.reshape(1, -1)
    scale = jnp.repeat(cell_scale, nodes_per_cell).reshape(1, -1)
    inv_root = inv_mass_root[None]
    potential = potential[None]
    boundary = boundary[None]
    width = boundary.shape[1]
    bands = lax.axis_size("band")
    odd = (lax.axis_index(SPACE[1]) % 2)[None]

    scaled, rim = pl.pallas_call(
        prepare_kernel,
        out_shape=(
            jax.ShapeDtypeStruct((rows, owned), BF),
            jax.ShapeDtypeStruct((rows, width), BF),
        ),
        name="prepare",
        compiler_params=pltpu.CompilerParams(vmem_limit_bytes=ROOM),
    )(states_in, inv_root, boundary)

    def operate(scaled, rim):
        chip = lax.all_gather(rim, SPACE[1], axis=0, axis_index_groups=[[0, 1], [2, 3]])
        across = with_chip(chip)
        held, _ = lax.optimization_barrier((scaled, chip))
        across, own = lax.optimization_barrier((across, own_gather(held, index, width)))
        past = with_core(across)
        terms, send, keep = cells(odd, own, across, chip, past, index, scale, kinetic, owned)
        partner = with_core(send)
        across = with_chip((keep.astype(F32) + partner[:2].astype(F32)).astype(BF))
        held, _ = lax.optimization_barrier((terms, partner))
        edge, own = lax.optimization_barrier((across[0], own_sum(held, index, owned, width)))
        past = with_core(edge)
        return own, partner, across, past

    arrived = operate(scaled, rim)
    first, scaled_first, rim = pl.pallas_call(
        first_kernel,
        out_shape=(
            jax.ShapeDtypeStruct((rows, owned), BF),
            jax.ShapeDtypeStruct((rows, owned), BF),
            jax.ShapeDtypeStruct((rows, width), BF),
        ),
        name="first",
        compiler_params=pltpu.CompilerParams(vmem_limit_bytes=ROOM),
    )(*arrived, scaled, states_in, inv_root, potential, boundary)
    arrived = operate(scaled_first, rim)
    filtered, blocks = pl.pallas_call(
        second_kernel,
        out_shape=(
            jax.ShapeDtypeStruct((rows, owned), BF),
            jax.ShapeDtypeStruct((bands, rows, owned // bands), BF),
        ),
        name="second",
        compiler_params=pltpu.CompilerParams(vmem_limit_bytes=ROOM),
    )(*arrived, scaled_first, states_in, first, inv_root, potential, boundary)

    outer = lax.axis_size(SPACE[0])
    node_total = owned * outer * QUAD
    regrouped = lax.all_to_all(blocks, "band", 0, 0, tiled=True).reshape(bands * rows, -1)
    partial_sum = lax.dot_general(regrouped, regrouped, (((1,), (1,)), ((), ())), preferred_element_type=F32)
    states = partial_sum.shape[0]
    blocks = partial_sum.astype(BF).reshape(bands * QUAD, states // (bands * QUAD), states)
    sums = lax.all_to_all(blocks, ("band", SPACE[1]), 0, 0, tiled=True).astype(F32).sum(axis=0)
    spread = jnp.broadcast_to(sums.astype(BF)[None], (outer, *sums.shape))
    total = lax.all_to_all(spread, SPACE[0], 0, 0, tiled=True).astype(F32).sum(axis=0)
    margin = lax.all_gather(total / node_total, SPACE[1], axis=0, tiled=True)
    return filtered, margin


def solution(mesh):
    bands = mesh.shape["band"]
    split = Mesh(mesh.devices.reshape(-1, QUAD, bands), (*SPACE, "band"))
    in_specs = (P("band", SPACE), P(), P(SPACE), P(None, SPACE), P(SPACE), P(SPACE), P(SPACE))
    out_specs = (P("band", SPACE), P("band", None))
    return jax.shard_map(body, mesh=split, in_specs=in_specs, out_specs=out_specs, check_vma=False)
```

```python
import jax
import jax.numpy as jnp
from jax import lax
from jax.experimental import pallas as pl
from jax.experimental.pallas import tpu as pltpu
from jax.sharding import Mesh
from jax.sharding import PartitionSpec as P

SPACE = ("outer", "quad")
QUAD = 4
OFFSETS = (-2, -1, 1, 2)
CENTER = 0.5
HALF = 6.0
TILE = 256
STEP = 2048
OWN_STEP = 4096
ROOM = 24 * 2**20
BF = jnp.bfloat16
F32 = jnp.float32


def selection(low, count):
    width = low.shape[1]
    lines = lax.broadcasted_iota(jnp.int32, (TILE, width), 0).astype(F32).astype(BF)
    place = (low % TILE).astype(F32)
    tiles = []
    for tile in range(count // TILE):
        here = jnp.where(low // TILE == tile, place, -1.0).astype(BF)
        tiles.append(jnp.where(lines == here, jnp.ones((), BF), jnp.zeros((), BF)))
    return jnp.concatenate(tiles, axis=0)


def picked(values, chosen):
    return jnp.dot(values, chosen, preferred_element_type=F32)


def put_back(values, chosen):
    return lax.dot_general(values, chosen, (((1,), (1,)), ((), ())), preferred_element_type=F32)


def from_pieces(values, piece, count):
    return jnp.concatenate([values[:, i * piece : (i + 1) * piece] for i in range(count)], axis=0)


def take_columns(values, index, piece):
    rows, count = values.shape[0], values.shape[1] // piece
    both = picked(from_pieces(values, piece, count), selection(index % piece, piece))
    part = index // piece
    result = both[:rows]
    for i in range(1, count):
        result = jnp.where(part == i, both[i * rows : (i + 1) * rows], result)
    return result


def add_columns(values, index, piece, count):
    rows = values.shape[0]
    part = index // piece
    none = jnp.zeros((), values.dtype)
    spread = jnp.concatenate([jnp.where(part == i, values, none) for i in range(count)], axis=0)
    sums = put_back(spread, selection(index % piece, piece))
    return [sums[i * rows : (i + 1) * rows] for i in range(count)]


def prepare_kernel(values, inv_root, boundary, scaled_ref, rim_ref):
    scaled = (inv_root[...] * values[...].astype(F32)).astype(BF)
    scaled_ref[...] = scaled
    rim_ref[...] = take_columns(scaled, boundary[...], boundary.shape[1]).astype(BF)


def slot(odd, i):
    return jnp.where(odd == 1, len(OFFSETS) - 1 - i, i)


def own_gather_kernel(index, scaled, out_ref, table):
    rows = scaled.shape[0]
    count, piece = table.shape[0] // rows, table.shape[1]

    @pl.when(pl.program_id(0) == 0)
    def _():
        table[...] = from_pieces(scaled[...], piece, count)

    places = index[...]
    part = places // piece
    both = picked(table[...], selection(places % piece, piece))
    gathered = jnp.zeros((), F32)
    for i in range(count):
        gathered = jnp.where(part == i, both[i * rows : (i + 1) * rows], gathered)
    out_ref[...] = gathered.astype(BF)


def own_gather(scaled, index, piece):
    rows, owned = scaled.shape
    places = index.shape[1]
    return pl.pallas_call(
        own_gather_kernel,
        grid=(places // OWN_STEP,),
        in_specs=[
            pl.BlockSpec((1, OWN_STEP), lambda i: (0, i)),
            pl.BlockSpec(scaled.shape, lambda i: (0, 0)),
        ],
        out_specs=pl.BlockSpec((rows, OWN_STEP), lambda i: (0, i)),
        out_shape=jax.ShapeDtypeStruct((rows, places), BF),
        scratch_shapes=[pltpu.VMEM((owned // piece * rows, piece), BF)],
        name="own_gather",
        compiler_params=pltpu.CompilerParams(vmem_limit_bytes=ROOM),
    )(index, scaled)


def cells_kernel(first, odd, index, scale, kinetic, own, chip, around, term_ref, send_ref, keep_ref, table, matrix, acc):
    step = pl.program_id(0)
    _, rows, piece = chip.shape
    count = len(OFFSETS)

    @pl.when(step == 0)
    def _():
        @pl.when(odd[0] == 0)
        def _():
            for i, ghosts in enumerate((around[0, 0], around[0, 1], chip[1], around[1, 0])):
                table[i * rows : (i + 1) * rows] = ghosts

        @pl.when(odd[0] == 1)
        def _():
            for i, ghosts in enumerate((around[0, 1], chip[0], around[1, 0], around[1, 1])):
                table[i * rows : (i + 1) * rows] = ghosts

        matrix[...] = jnp.zeros_like(matrix)
        nodes = kinetic.shape[0]
        for i in range(TILE // nodes):
            matrix[i * nodes : (i + 1) * nodes, i * nodes : (i + 1) * nodes] = kinetic[...]

    places = index[...]
    chosen = selection(places % piece, piece)
    part = places // piece - first
    both = picked(table[...], chosen)
    gathered = own[...].astype(F32)
    for i in range(count):
        gathered = jnp.where(part == i, both[i * rows : (i + 1) * rows], gathered)
    gathered = gathered.astype(BF)
    terms = jnp.concatenate(
        [put_back(gathered[:, i : i + TILE], matrix[...]) for i in range(0, STEP, TILE)], axis=1
    )
    terms = terms * scale[...]
    term_ref[...] = terms.astype(BF)
    spread = jnp.concatenate([jnp.where(part == i, terms, 0.0).astype(BF) for i in range(count)], axis=0)
    sums = put_back(spread, chosen)

    @pl.when(step == 0)
    def _():
        acc[...] = sums

    @pl.when(step > 0)
    def _():
        acc[...] += sums

    @pl.when(step == pl.num_programs(0) - 1)
    def _():
        def side(i):
            low = pl.multiple_of(slot(odd[0], i) * rows, rows)
            return acc[pl.ds(low, rows)].astype(BF)

        send_ref[0] = side(3)
        send_ref[1] = side(2)
        keep_ref[0] = side(0)
        keep_ref[1] = side(1)


def cells(odd, own, chip, around, index, scale, kinetic, owned):
    _, rows, piece = chip.shape
    places = index.shape[1]
    count = len(OFFSETS)

    def kernel(*refs):
        cells_kernel(owned // piece, *refs)

    line = pl.BlockSpec((1, STEP), lambda i, odd: (0, i))
    wide = pl.BlockSpec((rows, STEP), lambda i, odd: (0, i))

    def whole(shape):
        return pl.BlockSpec(shape, lambda i, odd: (0,) * len(shape))

    pair = (2, rows, piece)
    return pl.pallas_call(
        kernel,
        grid_spec=pltpu.PrefetchScalarGridSpec(
            num_scalar_prefetch=1,
            grid=(places // STEP,),
            in_specs=[line, line, whole(kinetic.shape), wide, whole(pair), whole(around.shape)],
            out_specs=[wide, whole(pair), whole(pair)],
            scratch_shapes=[pltpu.VMEM((count * rows, piece), BF), pltpu.VMEM((TILE, TILE), BF), pltpu.VMEM((count * rows, piece), F32)],
        ),
        out_shape=(
            jax.ShapeDtypeStruct((rows, places), BF),
            jax.ShapeDtypeStruct(pair, BF),
            jax.ShapeDtypeStruct(pair, BF),
        ),
        name="cells",
        compiler_params=pltpu.CompilerParams(vmem_limit_bytes=ROOM),
    )(odd, index, scale, kinetic, own, chip, around)


def own_sum_kernel(index, terms, out_ref, acc):
    step = pl.program_id(0)
    rows = terms.shape[0]
    piece = acc.shape[1]
    count = acc.shape[0] // rows
    places = index[...]
    part = places // piece
    values = terms[...].astype(F32)
    spread = jnp.concatenate([jnp.where(part == i, values, 0.0).astype(BF) for i in range(count)], axis=0)
    sums = put_back(spread, selection(places % piece, piece))

    @pl.when(step == 0)
    def _():
        acc[...] = sums

    @pl.when(step > 0)
    def _():
        acc[...] += sums

    @pl.when(step == pl.num_programs(0) - 1)
    def _():
        for i in range(count):
            out_ref[:, i * piece : (i + 1) * piece] = acc[i * rows : (i + 1) * rows]


def own_sum(terms, index, owned, piece):
    rows, places = terms.shape
    return pl.pallas_call(
        own_sum_kernel,
        grid=(places // OWN_STEP,),
        in_specs=[
            pl.BlockSpec((1, OWN_STEP), lambda i: (0, i)),
            pl.BlockSpec((rows, OWN_STEP), lambda i: (0, i)),
        ],
        out_specs=pl.BlockSpec((rows, owned), lambda i: (0, 0)),
        out_shape=jax.ShapeDtypeStruct((rows, owned), F32),
        scratch_shapes=[pltpu.VMEM((owned // piece * rows, piece), F32)],
        name="own_sum",
        compiler_params=pltpu.CompilerParams(vmem_limit_bytes=ROOM),
    )(index, terms)


def image_of(odd, own, chip, across, past, scaled, inv_root, potential, boundary):
    other = 1 - odd[0]
    back = chip[other, 1].astype(F32) + across[1].astype(F32) + past[other].astype(F32)
    upper = back.astype(BF)
    lower = (back - upper.astype(F32)).astype(BF)
    rows, piece = back.shape
    sums = add_columns(jnp.concatenate([upper, lower], axis=0), boundary[...], piece, own.shape[1] // piece)
    total = own[...] + jnp.concatenate([part[:rows] + part[rows:] for part in sums], axis=1)
    return inv_root[...] * (total + potential[...] * scaled[...].astype(F32))


def first_kernel(odd, own, chip, across, past, scaled, start, inv_root, potential, boundary, first_ref, scaled_ref, rim_ref):
    image = image_of(odd, own, chip, across, past, scaled, inv_root, potential, boundary)
    first = ((image - CENTER * start[...].astype(F32)) / HALF).astype(BF)
    first_ref[...] = first
    scaled_new = (inv_root[...] * first.astype(F32)).astype(BF)
    scaled_ref[...] = scaled_new
    rim_ref[...] = take_columns(scaled_new, boundary[...], boundary.shape[1]).astype(BF)


def second_kernel(odd, own, chip, across, past, scaled, start, first, inv_root, potential, boundary, out_ref, block_ref):
    image = image_of(odd, own, chip, across, past, scaled, inv_root, potential, boundary)
    second = 2.0 * (image - CENTER * first[...].astype(F32)) / HALF - start[...].astype(F32)
    second = second.astype(BF)
    out_ref[...] = second
    width = block_ref.shape[2]
    for i in range(block_ref.shape[0]):
        block_ref[i] = second[:, i * width : (i + 1) * width]


def of_chip(x):
    return lax.all_gather(x, SPACE[1], axis=0, axis_index_groups=[[0, 1], [2, 3]])


def with_chip(x):
    count = QUAD * lax.axis_size(SPACE[0])
    return lax.ppermute(x, SPACE, [(i, (i + 2 * (i % 2) - 1) % count) for i in range(count)])


def body(states_in, kinetic, cell_scale, cell_nodes, boundary, potential, inv_mass_root):
    nodes_per_cell = kinetic.shape[0]
    rows, owned = states_in.shape
    index = cell_nodes.T.reshape(1, -1)
    scale = jnp.repeat(cell_scale, nodes_per_cell).reshape(1, -1)
    inv_root = inv_mass_root[None]
    potential = potential[None]
    boundary = boundary[None]
    width = boundary.shape[1]
    bands = lax.axis_size("band")
    odd = (lax.axis_index(SPACE[1]) % 2)[None]

    scaled, rim = pl.pallas_call(
        prepare_kernel,
        out_shape=(
            jax.ShapeDtypeStruct((rows, owned), BF),
            jax.ShapeDtypeStruct((rows, width), BF),
        ),
        name="prepare",
        compiler_params=pltpu.CompilerParams(vmem_limit_bytes=ROOM),
    )(states_in, inv_root, boundary)

    def operate(scaled, rim):
        chip = of_chip(rim)
        across = with_chip(chip)
        held, _ = lax.optimization_barrier((scaled, chip))
        across, own = lax.optimization_barrier((across, own_gather(held, index, width)))
        terms, send, keep = cells(odd, own, chip, of_chip(across), index, scale, kinetic, owned)
        chip = of_chip(send)
        handed = lax.dynamic_index_in_dim(chip, 1 - odd[0], 0, keepdims=False)[:1]
        handed = jnp.pad(handed, ((1, 0), (0, 0), (0, 0)))
        across = with_chip((keep.astype(F32) + handed.astype(F32)).astype(BF))
        held, _ = lax.optimization_barrier((terms, chip))
        across, own = lax.optimization_barrier((across, own_sum(held, index, owned, width)))
        return odd, own, chip, across, of_chip(across[0])

    number = pl.BlockSpec(memory_space=pltpu.SMEM)
    array = pl.BlockSpec(memory_space=pltpu.VMEM)
    arrived = operate(scaled, rim)
    first, scaled_first, rim = pl.pallas_call(
        first_kernel,
        out_shape=(
            jax.ShapeDtypeStruct((rows, owned), BF),
            jax.ShapeDtypeStruct((rows, owned), BF),
            jax.ShapeDtypeStruct((rows, width), BF),
        ),
        in_specs=[number, *[array] * 9],
        name="first",
        compiler_params=pltpu.CompilerParams(vmem_limit_bytes=ROOM),
    )(*arrived, scaled, states_in, inv_root, potential, boundary)
    arrived = operate(scaled_first, rim)
    filtered, blocks = pl.pallas_call(
        second_kernel,
        out_shape=(
            jax.ShapeDtypeStruct((rows, owned), BF),
            jax.ShapeDtypeStruct((bands, rows, owned // bands), BF),
        ),
        in_specs=[number, *[array] * 10],
        name="second",
        compiler_params=pltpu.CompilerParams(vmem_limit_bytes=ROOM),
    )(*arrived, scaled_first, states_in, first, inv_root, potential, boundary)

    outer = lax.axis_size(SPACE[0])
    node_total = owned * outer * QUAD
    regrouped = lax.all_to_all(blocks, "band", 0, 0, tiled=True).reshape(bands * rows, -1)
    partial_sum = lax.dot_general(regrouped, regrouped, (((1,), (1,)), ((), ())), preferred_element_type=F32)
    states = partial_sum.shape[0]
    blocks = partial_sum.astype(BF).reshape(bands * QUAD, states // (bands * QUAD), states)
    sums = lax.all_to_all(blocks, ("band", SPACE[1]), 0, 0, tiled=True).astype(F32).sum(axis=0)
    spread = jnp.broadcast_to(sums.astype(BF)[None], (outer, *sums.shape))
    total = lax.all_to_all(spread, SPACE[0], 0, 0, tiled=True).astype(F32).sum(axis=0)
    margin = lax.all_gather(total / node_total, SPACE[1], axis=0, tiled=True)
    return filtered, margin


def solution(mesh):
    bands = mesh.shape["band"]
    split = Mesh(mesh.devices.reshape(-1, QUAD, bands), (*SPACE, "band"))
    in_specs = (P("band", SPACE), P(), P(SPACE), P(None, SPACE), P(SPACE), P(SPACE), P(SPACE))
    out_specs = (P("band", SPACE), P("band", None))
    return jax.shard_map(body, mesh=split, in_specs=in_specs, out_specs=out_specs, check_vma=False)
```

```python
import jax
import jax.numpy as jnp
from jax import lax
from jax.experimental import pallas as pl
from jax.experimental.pallas import tpu as pltpu
from jax.sharding import Mesh
from jax.sharding import PartitionSpec as P

SPACE = ("outer", "quad")
QUAD = 4
OFFSETS = (-2, -1, 1, 2)
CENTER = 0.5
HALF = 6.0
TILE = 256
STEP = 4096
OWN_STEP = 8192
ROOM = 24 * 2**20
BF = jnp.bfloat16
F32 = jnp.float32


def selection(low, count):
    width = low.shape[1]
    lines = lax.broadcasted_iota(jnp.int32, (TILE, width), 0).astype(F32).astype(BF)
    place = (low % TILE).astype(F32)
    tiles = []
    for tile in range(count // TILE):
        here = jnp.where(low // TILE == tile, place, -1.0).astype(BF)
        tiles.append(jnp.where(lines == here, jnp.ones((), BF), jnp.zeros((), BF)))
    return jnp.concatenate(tiles, axis=0)


def picked(values, chosen):
    return jnp.dot(values, chosen, preferred_element_type=F32)


def put_back(values, chosen):
    return lax.dot_general(values, chosen, (((1,), (1,)), ((), ())), preferred_element_type=F32)


def from_pieces(values, piece, count):
    return jnp.concatenate([values[:, i * piece : (i + 1) * piece] for i in range(count)], axis=0)


def take_columns(values, index, piece):
    rows, count = values.shape[0], values.shape[1] // piece
    both = picked(from_pieces(values, piece, count), selection(index % piece, piece))
    part = index // piece
    result = both[:rows]
    for i in range(1, count):
        result = jnp.where(part == i, both[i * rows : (i + 1) * rows], result)
    return result


def add_columns(values, index, piece, count):
    rows = values.shape[0]
    part = index // piece
    none = jnp.zeros((), values.dtype)
    spread = jnp.concatenate([jnp.where(part == i, values, none) for i in range(count)], axis=0)
    sums = put_back(spread, selection(index % piece, piece))
    return [sums[i * rows : (i + 1) * rows] for i in range(count)]


def prepare_kernel(values, inv_root, boundary, scaled_ref, rim_ref):
    scaled = (inv_root[...] * values[...].astype(F32)).astype(BF)
    scaled_ref[...] = scaled
    rim_ref[...] = take_columns(scaled, boundary[...], boundary.shape[1]).astype(BF)


def slot(odd, i):
    return jnp.where(odd == 1, len(OFFSETS) - 1 - i, i)


def own_gather_kernel(index, scaled, out_ref, table):
    rows = scaled.shape[0]
    count, piece = table.shape[0] // rows, table.shape[1]

    @pl.when(pl.program_id(0) == 0)
    def _():
        table[...] = from_pieces(scaled[...], piece, count)

    places = index[...]
    part = places // piece
    both = picked(table[...], selection(places % piece, piece))
    gathered = jnp.zeros((), F32)
    for i in range(count):
        gathered = jnp.where(part == i, both[i * rows : (i + 1) * rows], gathered)
    out_ref[...] = gathered.astype(BF)


def own_gather(scaled, index, piece):
    rows, owned = scaled.shape
    places = index.shape[1]
    return pl.pallas_call(
        own_gather_kernel,
        grid=(places // OWN_STEP,),
        in_specs=[
            pl.BlockSpec((1, OWN_STEP), lambda i: (0, i)),
            pl.BlockSpec(scaled.shape, lambda i: (0, 0)),
        ],
        out_specs=pl.BlockSpec((rows, OWN_STEP), lambda i: (0, i)),
        out_shape=jax.ShapeDtypeStruct((rows, places), BF),
        scratch_shapes=[pltpu.VMEM((owned // piece * rows, piece), BF)],
        name="own_gather",
        compiler_params=pltpu.CompilerParams(vmem_limit_bytes=ROOM),
    )(index, scaled)


def cells_kernel(first, odd, index, scale, kinetic, own, chip, around, term_ref, send_ref, keep_ref, table, matrix, acc):
    step = pl.program_id(0)
    _, rows, piece = chip.shape
    count = len(OFFSETS)

    @pl.when(step == 0)
    def _():
        @pl.when(odd[0] == 0)
        def _():
            for i, ghosts in enumerate((around[0, 0], around[0, 1], chip[1], around[1, 0])):
                table[i * rows : (i + 1) * rows] = ghosts

        @pl.when(odd[0] == 1)
        def _():
            for i, ghosts in enumerate((around[0, 1], chip[0], around[1, 0], around[1, 1])):
                table[i * rows : (i + 1) * rows] = ghosts

        matrix[...] = jnp.zeros_like(matrix)
        nodes = kinetic.shape[0]
        for i in range(TILE // nodes):
            matrix[i * nodes : (i + 1) * nodes, i * nodes : (i + 1) * nodes] = kinetic[...]

    places = index[...]
    chosen = selection(places % piece, piece)
    part = places // piece - first
    both = picked(table[...], chosen)
    gathered = own[...].astype(F32)
    for i in range(count):
        gathered = jnp.where(part == i, both[i * rows : (i + 1) * rows], gathered)
    gathered = gathered.astype(BF)
    terms = jnp.concatenate(
        [put_back(gathered[:, i : i + TILE], matrix[...]) for i in range(0, STEP, TILE)], axis=1
    )
    terms = terms * scale[...]
    term_ref[...] = terms.astype(BF)
    spread = jnp.concatenate([jnp.where(part == i, terms, 0.0).astype(BF) for i in range(count)], axis=0)
    sums = put_back(spread, chosen)

    @pl.when(step == 0)
    def _():
        acc[...] = sums

    @pl.when(step > 0)
    def _():
        acc[...] += sums

    @pl.when(step == pl.num_programs(0) - 1)
    def _():
        def side(i):
            low = pl.multiple_of(slot(odd[0], i) * rows, rows)
            return acc[pl.ds(low, rows)].astype(BF)

        send_ref[0] = side(3)
        send_ref[1] = side(2)
        keep_ref[0] = side(0)
        keep_ref[1] = side(1)


def cells(odd, own, chip, around, index, scale, kinetic, owned):
    _, rows, piece = chip.shape
    places = index.shape[1]
    count = len(OFFSETS)

    def kernel(*refs):
        cells_kernel(owned // piece, *refs)

    line = pl.BlockSpec((1, STEP), lambda i, odd: (0, i))
    wide = pl.BlockSpec((rows, STEP), lambda i, odd: (0, i))

    def whole(shape):
        return pl.BlockSpec(shape, lambda i, odd: (0,) * len(shape))

    pair = (2, rows, piece)
    return pl.pallas_call(
        kernel,
        grid_spec=pltpu.PrefetchScalarGridSpec(
            num_scalar_prefetch=1,
            grid=(places // STEP,),
            in_specs=[line, line, whole(kinetic.shape), wide, whole(pair), whole(around.shape)],
            out_specs=[wide, whole(pair), whole(pair)],
            scratch_shapes=[pltpu.VMEM((count * rows, piece), BF), pltpu.VMEM((TILE, TILE), BF), pltpu.VMEM((count * rows, piece), F32)],
        ),
        out_shape=(
            jax.ShapeDtypeStruct((rows, places), BF),
            jax.ShapeDtypeStruct(pair, BF),
            jax.ShapeDtypeStruct(pair, BF),
        ),
        name="cells",
        compiler_params=pltpu.CompilerParams(vmem_limit_bytes=ROOM),
    )(odd, index, scale, kinetic, own, chip, around)


def own_sum_kernel(index, terms, out_ref, acc):
    step = pl.program_id(0)
    rows = terms.shape[0]
    piece = acc.shape[1]
    count = acc.shape[0] // rows
    places = index[...]
    part = places // piece
    values = terms[...].astype(F32)
    spread = jnp.concatenate([jnp.where(part == i, values, 0.0).astype(BF) for i in range(count)], axis=0)
    sums = put_back(spread, selection(places % piece, piece))

    @pl.when(step == 0)
    def _():
        acc[...] = sums

    @pl.when(step > 0)
    def _():
        acc[...] += sums

    @pl.when(step == pl.num_programs(0) - 1)
    def _():
        for i in range(count):
            out_ref[:, i * piece : (i + 1) * piece] = acc[i * rows : (i + 1) * rows]


def own_sum(terms, index, owned, piece):
    rows, places = terms.shape
    return pl.pallas_call(
        own_sum_kernel,
        grid=(places // OWN_STEP,),
        in_specs=[
            pl.BlockSpec((1, OWN_STEP), lambda i: (0, i)),
            pl.BlockSpec((rows, OWN_STEP), lambda i: (0, i)),
        ],
        out_specs=pl.BlockSpec((rows, owned), lambda i: (0, 0)),
        out_shape=jax.ShapeDtypeStruct((rows, owned), F32),
        scratch_shapes=[pltpu.VMEM((owned // piece * rows, piece), F32)],
        name="own_sum",
        compiler_params=pltpu.CompilerParams(vmem_limit_bytes=ROOM),
    )(index, terms)


def image_of(odd, own, chip, across, past, scaled, inv_root, potential, boundary):
    other = 1 - odd[0]
    back = chip[other, 1].astype(F32) + across[1].astype(F32) + past[other].astype(F32)
    upper = back.astype(BF)
    lower = (back - upper.astype(F32)).astype(BF)
    rows, piece = back.shape
    sums = add_columns(jnp.concatenate([upper, lower], axis=0), boundary[...], piece, own.shape[1] // piece)
    total = own[...] + jnp.concatenate([part[:rows] + part[rows:] for part in sums], axis=1)
    return inv_root[...] * (total + potential[...] * scaled[...].astype(F32))


def first_kernel(odd, own, chip, across, past, scaled, start, inv_root, potential, boundary, first_ref, scaled_ref, rim_ref):
    image = image_of(odd, own, chip, across, past, scaled, inv_root, potential, boundary)
    first = ((image - CENTER * start[...].astype(F32)) / HALF).astype(BF)
    first_ref[...] = first
    scaled_new = (inv_root[...] * first.astype(F32)).astype(BF)
    scaled_ref[...] = scaled_new
    rim_ref[...] = take_columns(scaled_new, boundary[...], boundary.shape[1]).astype(BF)


def second_kernel(odd, own, chip, across, past, scaled, start, first, inv_root, potential, boundary, out_ref, block_ref):
    image = image_of(odd, own, chip, across, past, scaled, inv_root, potential, boundary)
    second = 2.0 * (image - CENTER * first[...].astype(F32)) / HALF - start[...].astype(F32)
    second = second.astype(BF)
    out_ref[...] = second
    width = block_ref.shape[2]
    for i in range(block_ref.shape[0]):
        block_ref[i] = second[:, i * width : (i + 1) * width]


def of_chip(x):
    return lax.all_gather(x, SPACE[1], axis=0, axis_index_groups=[[0, 1], [2, 3]])


def with_chip(x):
    count = QUAD * lax.axis_size(SPACE[0])
    return lax.ppermute(x, SPACE, [(i, (i + 2 * (i % 2) - 1) % count) for i in range(count)])


def body(states_in, kinetic, cell_scale, cell_nodes, boundary, potential, inv_mass_root):
    nodes_per_cell = kinetic.shape[0]
    rows, owned = states_in.shape
    index = cell_nodes.T.reshape(1, -1)
    scale = jnp.repeat(cell_scale, nodes_per_cell).reshape(1, -1)
    inv_root = inv_mass_root[None]
    potential = potential[None]
    boundary = boundary[None]
    width = boundary.shape[1]
    bands = lax.axis_size("band")
    odd = (lax.axis_index(SPACE[1]) % 2)[None]

    scaled, rim = pl.pallas_call(
        prepare_kernel,
        out_shape=(
            jax.ShapeDtypeStruct((rows, owned), BF),
            jax.ShapeDtypeStruct((rows, width), BF),
        ),
        name="prepare",
        compiler_params=pltpu.CompilerParams(vmem_limit_bytes=ROOM),
    )(states_in, inv_root, boundary)

    def operate(scaled, rim):
        chip = of_chip(rim)
        across = with_chip(chip)
        held, _ = lax.optimization_barrier((scaled, chip))
        across, own = lax.optimization_barrier((across, own_gather(held, index, width)))
        terms, send, keep = cells(odd, own, chip, of_chip(across), index, scale, kinetic, owned)
        chip = of_chip(send)
        handed = lax.dynamic_index_in_dim(chip, 1 - odd[0], 0, keepdims=False)[:1]
        handed = jnp.pad(handed, ((1, 0), (0, 0), (0, 0)))
        across = with_chip((keep.astype(F32) + handed.astype(F32)).astype(BF))
        held, _ = lax.optimization_barrier((terms, chip))
        across, own = lax.optimization_barrier((across, own_sum(held, index, owned, width)))
        return odd, own, chip, across, of_chip(across[0])

    number = pl.BlockSpec(memory_space=pltpu.SMEM)
    array = pl.BlockSpec(memory_space=pltpu.VMEM)
    arrived = operate(scaled, rim)
    first, scaled_first, rim = pl.pallas_call(
        first_kernel,
        out_shape=(
            jax.ShapeDtypeStruct((rows, owned), BF),
            jax.ShapeDtypeStruct((rows, owned), BF),
            jax.ShapeDtypeStruct((rows, width), BF),
        ),
        in_specs=[number, *[array] * 9],
        name="first",
        compiler_params=pltpu.CompilerParams(vmem_limit_bytes=ROOM),
    )(*arrived, scaled, states_in, inv_root, potential, boundary)
    arrived = operate(scaled_first, rim)
    filtered, blocks = pl.pallas_call(
        second_kernel,
        out_shape=(
            jax.ShapeDtypeStruct((rows, owned), BF),
            jax.ShapeDtypeStruct((bands, rows, owned // bands), BF),
        ),
        in_specs=[number, *[array] * 10],
        name="second",
        compiler_params=pltpu.CompilerParams(vmem_limit_bytes=ROOM),
    )(*arrived, scaled_first, states_in, first, inv_root, potential, boundary)

    outer = lax.axis_size(SPACE[0])
    node_total = owned * outer * QUAD
    regrouped = lax.all_to_all(blocks, "band", 0, 0, tiled=True).reshape(bands * rows, -1)
    partial_sum = lax.dot_general(regrouped, regrouped, (((1,), (1,)), ((), ())), preferred_element_type=F32)
    states = partial_sum.shape[0]
    blocks = partial_sum.astype(BF).reshape(bands * QUAD, states // (bands * QUAD), states)
    sums = lax.all_to_all(blocks, ("band", SPACE[1]), 0, 0, tiled=True).astype(F32).sum(axis=0)
    spread = jnp.broadcast_to(sums.astype(BF)[None], (outer, *sums.shape))
    total = lax.all_to_all(spread, SPACE[0], 0, 0, tiled=True).astype(F32).sum(axis=0)
    margin = lax.all_gather(total / node_total, SPACE[1], axis=0, tiled=True)
    return filtered, margin


def solution(mesh):
    bands = mesh.shape["band"]
    split = Mesh(mesh.devices.reshape(-1, QUAD, bands), (*SPACE, "band"))
    in_specs = (P("band", SPACE), P(), P(SPACE), P(None, SPACE), P(SPACE), P(SPACE), P(SPACE))
    out_specs = (P("band", SPACE), P("band", None))
    return jax.shard_map(body, mesh=split, in_specs=in_specs, out_specs=out_specs, check_vma=False)
```
